32 devices in a mesh: leaf: 16 (over z, y, x), panel: 2 (over core).
Axes of the slice: x: 2, y: 2, z: 4, core: 2. Of those that a mesh axis runs over, the one named last changes fastest.
Arguments:
- child_front: bfloat16 [4096, 16384], P('leaf', 'panel'), may hold values from -6 to 6
- own_map: int32 [3, 16, 2], P(None, 'leaf'), may hold values from 0 to 1, each once within a row
- cross_map: int32 [3, 16, 2], P(None, 'leaf'), may hold values from 0 to 1, each once within a row
- pivot_inverse: bfloat16 [7, 512, 512], replicated, may hold values from -0.0029296875 to 0.0029296875
Outputs:
- schur: bfloat16 [4096, 16384], P('leaf', 'panel')
The draws below stay inside these ranges and needn't reach their ends.
Inputs may be any that keep to these rules, and one draw needn't show every extreme that they name: Each own_map[k, d, :] is a permutation of the 2 blocks. Each cross_map[k, d, :] is a permutation of the 2 blocks.
All inputs are finite; a program needn't handle non-finite values.
Results may differ from the reference program's by a relative error of at most 0.0088.
Values may be sent and summed in bfloat16 or wider, within the bound.
No kernel may reach another device: no remote copies, remote signals or barrier semaphores. Data moves between devices by JAX's collectives and lax.ppermute only.
A program may use at most 64 MiB of HBM per device.

```python
import jax
import jax.numpy as jnp
from jax import lax

NF = 16384
PANEL = 512
BLOCK = 128
LEVELS = 3
INVERSES = 7
ROWS_DEV = 256
NB = 2
LEAF_BITS = 4
FRONT_ROWS = 4096
N_LEAF = 16


def steps_of(own_key, dims, pieces, low, high):
    loudness, own = 1.0, jax.random.fold_in(own_key, 6)
    for position, blocks in pieces:
        heights = jnp.exp(jax.random.uniform(jax.random.fold_in(own, position), (blocks,), jnp.float32, low / len(pieces), high / len(pieces)))
        loudness = loudness * jnp.repeat(heights, dims[position] // blocks).reshape([-1 if axis == position else 1 for axis in range(len(dims))])
    return loudness


def bell_draw(key, dims, scale, reach, shards=(), kind=jnp.bfloat16):
    factor_of = steps_of(key, dims, shards, -0.22, 0.18) if shards else 1.0
    drawn = jax.random.normal(key, dims, jnp.float32) * scale * factor_of
    return jnp.minimum(jnp.maximum(drawn, -reach), reach).astype(kind)


def setup_inputs(seed: int = 0) -> dict:
    arg_keys = jax.random.split(jax.random.key(seed), 5)
    return {
        "child_front": bell_draw(arg_keys[0], (FRONT_ROWS, NF), 1.0, 6.0, ((0, 16), (1, 2))),
        "own_map": jax.vmap(lambda own: jax.random.permutation(own, NB))(jax.random.split(arg_keys[1], LEVELS * N_LEAF)).reshape((LEVELS, N_LEAF, NB)).astype(jnp.int32),
        "cross_map": jax.vmap(lambda own: jax.random.permutation(own, NB))(jax.random.split(arg_keys[2], LEVELS * N_LEAF)).reshape((LEVELS, N_LEAF, NB)).astype(jnp.int32),
        "pivot_inverse": bell_draw(arg_keys[3], (INVERSES, PANEL, PANEL), (16 * PANEL * PANEL) ** -0.5, 0.0029296875),
    }


def reference(child_front, own_map, cross_map, pivot_inverse):
    leaf_count = N_LEAF
    front_slab = child_front
    offsets = (0, 4, 6)
    for level_index in range(3):
        group_size = leaf_count // 2 ** (2 - level_index)
        share_rows = PANEL // group_size
        sibling_bit = LEAF_BITS - 3 + level_index
        blocks = front_slab.reshape(leaf_count, NB, BLOCK, NF)
        partner = jnp.take(blocks, jnp.arange(leaf_count, dtype=jnp.int32) ^ (1 << sibling_bit), axis=0)
        own_part = jnp.take_along_axis(blocks, own_map[level_index][:, :, None, None].astype(jnp.int32), axis=1)
        cross_part = jnp.take_along_axis(partner, cross_map[level_index][:, :, None, None].astype(jnp.int32), axis=1)
        parent = (own_part.astype(jnp.float32) + cross_part.astype(jnp.float32)).astype(jnp.bfloat16)
        parent = parent.reshape(leaf_count, ROWS_DEV, NF)
        fronts = leaf_count // group_size
        pivots = parent[:, :share_rows, :].reshape(fronts, PANEL, NF)
        inverse = pivot_inverse[offsets[level_index]:offsets[level_index] + fronts]

        def solve_one(operands):
            return jnp.dot(operands[0], operands[1], preferred_element_type=jnp.float32).astype(jnp.bfloat16)

        upper_rows = lax.map(solve_one, (inverse, pivots))

        def update(device):
            slab_rows = parent[device]
            upper_now = upper_rows[device // group_size]
            reduced = slab_rows.astype(jnp.float32) - jnp.dot(slab_rows[:, :PANEL], upper_now, preferred_element_type=jnp.float32)
            keep_mask = jnp.arange(ROWS_DEV, dtype=jnp.int32)[:, None] >= share_rows
            return jnp.where(keep_mask, reduced, jnp.zeros_like(reduced)).astype(jnp.bfloat16)

        front_slab = lax.map(update, jnp.arange(leaf_count, dtype=jnp.int32)).reshape(leaf_count * ROWS_DEV, NF)
    return front_slab
```

```python
import functools

import jax
import jax.numpy as jnp
from jax import lax
from jax.experimental import pallas as pl
from jax.experimental.pallas import tpu as pltpu
from jax.sharding import PartitionSpec as P

PANEL = 512
BLOCK = 128
MAP_ROWS = 16
MAP_COLS = 12
CHUNKS = 1
TILE = 256

F32 = jnp.float32
BF16 = jnp.bfloat16


def xor_leaf(block, mask):
    count = lax.axis_size("leaf")
    return lax.ppermute(block, "leaf", [(i, i ^ mask) for i in range(count)])


def dot(a, b):
    return jnp.dot(a, b, preferred_element_type=F32)


def vmem():
    return pl.BlockSpec(memory_space=pltpu.VMEM)


def smem():
    return pl.BlockSpec(memory_space=pltpu.SMEM)


def anywhere():
    return pl.BlockSpec(memory_space=pl.ANY)


def block_at(index):
    return pl.ds(pl.multiple_of(index * BLOCK, BLOCK), BLOCK)


def own_at(level, slot):
    return 2 * level + slot


def cross_at(level, slot):
    return 6 + 2 * level + slot


def lead_level0_kernel(share, maps, near, inverse, left, seed, pivots):
    group = near.shape[0]
    rows = 2 * BLOCK
    rest = rows - share
    for r in range(group):
        sibling = r ^ (group // 2)
        for s in range(2):
            own = near[r, block_at(maps[r, own_at(0, s)]), :].astype(F32)
            cross = near[sibling, block_at(maps[r, cross_at(0, s)]), :].astype(F32)
            summed = (own + cross).astype(BF16)
            if s == 0:
                pivots[r * share:(r + 1) * share, :] = summed[:share]
                if share < BLOCK:
                    left[r * rest:r * rest + BLOCK - share, :] = summed[share:]
            else:
                left[r * rest + BLOCK - share:(r + 1) * rest, :] = summed
    upper = dot(inverse[...], pivots[...]).astype(BF16)
    mine = left[0:rest, :]
    seed[...] = (mine.astype(F32) - dot(mine, upper)).astype(BF16)


def lead_level12_kernel(gone, share, keep, parts, meta, maps, *refs):
    gathered = refs[:parts]
    inverse, left1, left2, front, pivots, upper, sems = refs[parts:]
    group, planes = gathered[0].shape[0], gathered[0].shape[1]
    width = gathered[0].shape[3]
    slabs = group * planes
    rows = 2 * BLOCK
    rest = rows - share
    last = rows - keep
    copies = []
    for i in range(parts):
        column = pl.multiple_of((meta[0] ^ i) * width, width)
        for h in range(planes):
            copy = pltpu.make_async_copy(
                gathered[i].at[:, h, pl.ds(0, rows - gone), :],
                front.at[pl.ds(h * group, group), pl.ds(gone, rows - gone), pl.ds(column, width)],
                sems.at[i * planes + h],
            )
            copy.start()
            copies.append(copy)
    front[:, 0:gone, :] = jnp.zeros((slabs, gone, PANEL), BF16)
    for copy in copies:
        copy.wait()

    def extend1(slab, carry):
        sibling = slab ^ group
        base = slab * rest
        for s in range(2):
            own = front[slab, block_at(maps[slab, own_at(1, s)]), :].astype(F32)
            cross = front[sibling, block_at(maps[slab, cross_at(1, s)]), :].astype(F32)
            summed = (own + cross).astype(BF16)
            if s == 0:
                pivots[pl.ds(pl.multiple_of(slab * share, 16), share), :] = summed[:share]
                left1[pl.ds(pl.multiple_of(base, 16), BLOCK - share), :] = summed[share:]
            else:
                left1[pl.ds(pl.multiple_of(base + BLOCK - share, 16), BLOCK), :] = summed
        return carry

    lax.fori_loop(0, slabs, extend1, 0)
    for half in range(2):
        upper[...] = dot(inverse[half], pivots[half * PANEL:(half + 1) * PANEL, :]).astype(BF16)

        def reduce1(pair, carry):
            first = half * (slabs // 2) + 2 * pair
            mine = left1[pl.ds(pl.multiple_of(first * rest, 16), 2 * rest), :]
            reduced = (mine.astype(F32) - dot(mine, upper[...])).astype(BF16)
            front[first, share:rows, :] = reduced[:rest]
            front[first + 1, share:rows, :] = reduced[rest:]
            return carry

        lax.fori_loop(0, slabs // 4, reduce1, 0)

    def extend2(slab, carry):
        sibling = slab + slabs // 2
        base = slab * last
        for s in range(2):
            own = front[slab, block_at(maps[slab, own_at(2, s)]), :].astype(F32)
            cross = front[sibling, block_at(maps[slab, cross_at(2, s)]), :].astype(F32)
            summed = (own + cross).astype(BF16)
            if s == 0:
                left2[pl.ds(pl.multiple_of(base, 16), BLOCK - keep), :] = summed[keep:]
            else:
                left2[pl.ds(pl.multiple_of(base + BLOCK - keep, 16), BLOCK), :] = summed
        return carry

    lax.fori_loop(0, slabs // 2, extend2, 0)


def level0_kernel(share, meta, maps, *refs):
    group = refs[-1].shape[0]
    slabs = refs[:group]
    left, inverse, out, parent = refs[group:]
    rows = 2 * BLOCK
    rest = rows - share
    tile = out.shape[2]
    for r in range(group):
        sibling = slabs[r ^ (group // 2)]
        for s in range(2):
            own = slabs[r][block_at(maps[r, own_at(0, s)]), :].astype(F32)
            cross = sibling[block_at(maps[r, cross_at(0, s)]), :].astype(F32)
            parent[r, s * BLOCK:(s + 1) * BLOCK, :] = (own + cross).astype(BF16)
    pivots = parent[:, 0:share, :].reshape(PANEL, tile)
    upper = dot(inverse[...], pivots).astype(BF16)
    product = dot(left[...], upper)
    for r in range(group):
        kept = parent[r, share:rows, :].astype(F32)
        out[r, :, :] = (kept - product[r * rest:(r + 1) * rest]).astype(BF16)


def level12_kernel(gone, share, final, keep, maps, *refs):
    planes = refs[:4]
    left1, inverse1, left2, inverse2 = refs[4:8]
    outs = refs[8:-5]
    front, parent, nextf, upper, pivots = refs[-5:]
    group = planes[0].shape[0]
    slabs = 4 * group
    tile = planes[0].shape[2]
    rows = 2 * BLOCK
    rest = rows - share
    last = rows - keep

    @pl.when(pl.program_id(0) == 0)
    def _():
        front[:, 0:gone, :] = jnp.zeros((slabs, gone, tile), BF16)
        nextf[:, 0:share, :] = jnp.zeros((slabs, share, tile), BF16)

    for h in range(4):
        front[h * group:(h + 1) * group, gone:rows, :] = planes[h][...]

    def extend1(slab, carry):
        sibling = slab ^ group
        for s in range(2):
            own = front[slab, block_at(maps[slab, own_at(1, s)]), :].astype(F32)
            cross = front[sibling, block_at(maps[slab, cross_at(1, s)]), :].astype(F32)
            parent[slab, s * BLOCK:(s + 1) * BLOCK, :] = (own + cross).astype(BF16)
        return carry

    lax.fori_loop(0, slabs, extend1, 0)
    for half in range(2):
        taken = parent[half * 2 * group:(half + 1) * 2 * group, 0:share, :].reshape(PANEL, tile)
        upper[...] = dot(inverse1[half], taken).astype(BF16)

        def reduce1(quad, carry):
            first = half * 2 * group + 4 * quad
            product = dot(left1[pl.ds(pl.multiple_of(first * rest, 16), 4 * rest), :], upper[...])
            for i in range(4):
                kept = parent[first + i, share:rows, :].astype(F32)
                nextf[first + i, share:rows, :] = (kept - product[i * rest:(i + 1) * rest]).astype(BF16)
            return carry

        lax.fori_loop(0, group // 2, reduce1, 0)

    def extend2(slab, carry):
        sibling = slab + 2 * group
        for s in range(2):
            own = nextf[slab, block_at(maps[slab, own_at(2, s)]), :].astype(F32)
            cross = nextf[sibling, block_at(maps[slab, cross_at(2, s)]), :].astype(F32)
            parent[slab, s * BLOCK:(s + 1) * BLOCK, :] = (own + cross).astype(BF16)
        return carry

    lax.fori_loop(0, 2 * group, extend2, 0)
    head = max(final, 16)
    for slab in range(slabs):
        if slab < 2 * group:
            taken = parent[slab, 0:head, :]
        else:
            at = pl.multiple_of(maps[slab, own_at(2, 0)] * BLOCK, BLOCK)
            own = nextf[slab, pl.ds(at, head), :].astype(F32)
            at = pl.multiple_of(maps[slab, cross_at(2, 0)] * BLOCK, BLOCK)
            cross = nextf[slab - 2 * group, pl.ds(at, head), :].astype(F32)
            taken = (own + cross).astype(BF16)
        pivots[slab * final:(slab + 1) * final, :] = taken.astype(pivots.dtype)[:final]
    upper[...] = dot(inverse2[...], pivots[...].astype(BF16)).astype(BF16)
    for slab in range(2 * group):
        product = dot(left2[slab * last:(slab + 1) * last, :], upper[...])
        reduced = parent[slab, keep:rows, :].astype(F32) - product
        if keep < final:
            row = lax.broadcasted_iota(jnp.int32, reduced.shape, 0)
            reduced = jnp.where(row >= final - keep, reduced, 0.0)
        outs[slab][...] = reduced.astype(BF16)


def place_kernel(keep, count, meta, *refs):
    pieces, out = refs[:count], refs[-1]
    if keep:
        out[0:keep, :] = jnp.zeros((keep, out.shape[1]), BF16)
    for i, piece in enumerate(pieces):

        @pl.when(pl.program_id(0) == i)
        def _(piece=piece):
            out[keep:, :] = piece[...]


def reordered(inverse, shift):
    index = jnp.arange(PANEL, dtype=jnp.int32)
    table = (index[:, None] == (index[None, :] ^ shift)).astype(BF16)
    return dot(inverse, table).astype(BF16)


def on_device(child_front, own_map, cross_map, pivot_inverse):
    leaf_count = lax.axis_size("leaf")
    panel_count = lax.axis_size("panel")
    leaf = lax.axis_index("leaf")
    panel = lax.axis_index("panel")
    rows, cols = child_front.shape
    group = leaf_count // 4
    member, plane = leaf % group, leaf // group
    half = plane & 1
    share0, share1, share2 = (PANEL // (group << k) for k in range(3))
    keep = share2 // 16 * 16
    span = cols // group
    chunks = min(CHUNKS, span // (2 * BLOCK))
    chunk = span // chunks
    side = chunk // 2
    tile = min(TILE, side)

    maps = jnp.concatenate([own_map[:, 0, :], cross_map[:, 0, :]], axis=0).reshape(1, MAP_COLS)
    map_rows = jnp.pad(maps.astype(BF16), ((0, MAP_ROWS - 1), (0, PANEL - MAP_COLS)))
    lead = jnp.concatenate([child_front[:, :PANEL], map_rows], axis=0)
    near = [lead]
    for r in range(1, group):
        pairs = [(i * panel_count, (i ^ r) * panel_count) for i in range(leaf_count)]
        near.append(lax.ppermute(lead, ("leaf", "panel"), pairs))
    near = jnp.stack(near)
    first = near
    for p in range(1, panel_count):
        near = jnp.where(panel == p, lax.ppermute(first, "panel", [(0, p)]), near)
    near_maps = near[:, rows, :MAP_COLS].astype(jnp.int32)

    pick = functools.partial(lax.dynamic_index_in_dim, pivot_inverse, axis=0, keepdims=False)
    inverse0 = reordered(pick(plane), member * share0)
    low = (leaf % (2 * group)) * share1
    inverse1 = jnp.stack([reordered(pick(4 + ((plane >> 1) ^ i)), low) for i in range(2)])
    inverse2 = reordered(pivot_inverse[6], leaf * share2)

    received = []
    for k in range(chunks):
        parts = []
        for r in range(1, group):
            start = (member ^ r) * span + k * chunk
            parts.append(xor_leaf(lax.dynamic_slice(child_front, (0, start), (rows, chunk)), r))
        received.append(parts)

    rest0, rest1, last = rows - share0, rows - share1, rows - keep
    left0, seed = pl.pallas_call(
        functools.partial(lead_level0_kernel, share0),
        out_shape=(
            jax.ShapeDtypeStruct((group * rest0, PANEL), BF16),
            jax.ShapeDtypeStruct((rest0, PANEL), BF16),
        ),
        in_specs=[smem(), vmem(), vmem()],
        out_specs=(vmem(), vmem()),
        scratch_shapes=[pltpu.VMEM((PANEL, PANEL), BF16)],
        name="lead0",
    )(near_maps, near, inverse0)

    width = PANEL // panel_count
    piece = lax.dynamic_slice(seed, (0, panel * width), (rest0, width))
    piece = jnp.concatenate([piece, map_rows[:, :width]], axis=0)
    piece = jnp.stack([piece] + [xor_leaf(piece, m * group) for m in range(1, 4)])
    piece = jnp.stack([piece] + [xor_leaf(piece, r) for r in range(1, group)])
    gathered = [piece]
    for i in range(1, panel_count):
        gathered.append(lax.ppermute(piece, "panel", [(p, p ^ i) for p in range(panel_count)]))
    all_maps = piece[:, :, rest0, :MAP_COLS].transpose(1, 0, 2).reshape(leaf_count, MAP_COLS)
    all_maps = all_maps.astype(jnp.int32)

    left1, left2 = pl.pallas_call(
        functools.partial(lead_level12_kernel, share0, share1, keep, panel_count),
        out_shape=(
            jax.ShapeDtypeStruct((leaf_count * rest1, PANEL), BF16),
            jax.ShapeDtypeStruct((2 * group * last, PANEL), BF16),
        ),
        in_specs=[smem(), smem()] + [anywhere()] * panel_count + [vmem()],
        out_specs=(vmem(), vmem()),
        scratch_shapes=[
            pltpu.VMEM((leaf_count, rows, PANEL), BF16),
            pltpu.VMEM((2 * PANEL, PANEL), BF16),
            pltpu.VMEM((PANEL, PANEL), BF16),
            pltpu.SemaphoreType.DMA((4 * panel_count,)),
        ],
        name="lead12",
    )(panel.reshape(1), all_maps, *gathered, inverse1)

    def level0(k, which):
        own_block = (member * span + k * chunk + which * side) // tile
        meta = jnp.stack([own_block, which * (side // tile)]).astype(jnp.int32)
        return pl.pallas_call(
            functools.partial(level0_kernel, share0),
            out_shape=jax.ShapeDtypeStruct((group, rest0, side), BF16),
            grid_spec=pltpu.PrefetchScalarGridSpec(
                num_scalar_prefetch=2,
                grid=(side // tile,),
                in_specs=[pl.BlockSpec((rows, tile), lambda j, meta, maps: (0, meta[0] + j))]
                + [pl.BlockSpec((rows, tile), lambda j, meta, maps: (0, meta[1] + j))] * (group - 1)
                + [
                    pl.BlockSpec((group * rest0, PANEL), lambda j, meta, maps: (0, 0)),
                    pl.BlockSpec((PANEL, PANEL), lambda j, meta, maps: (0, 0)),
                ],
                out_specs=pl.BlockSpec((group, rest0, tile), lambda j, meta, maps: (0, 0, j)),
                scratch_shapes=[pltpu.VMEM((group, rows, tile), BF16)],
            ),
            name="level0",
        )(meta, near_maps, child_front, *received[k], left0, inverse0)

    def level12(planes):
        return pl.pallas_call(
            functools.partial(level12_kernel, share0, share1, share2, keep),
            out_shape=[jax.ShapeDtypeStruct((last, side), BF16)] * (2 * group),
            grid_spec=pltpu.PrefetchScalarGridSpec(
                num_scalar_prefetch=1,
                grid=(side // tile,),
                in_specs=[pl.BlockSpec((group, rest0, tile), lambda j, maps: (0, 0, j))] * 4 + [vmem()] * 4,
                out_specs=[pl.BlockSpec((last, tile), lambda j, maps: (0, j))] * (2 * group),
                scratch_shapes=[
                    pltpu.VMEM((leaf_count, rows, tile), BF16),
                    pltpu.VMEM((leaf_count, rows, tile), BF16),
                    pltpu.VMEM((leaf_count, rows, tile), BF16),
                    pltpu.VMEM((PANEL, tile), BF16),
                    pltpu.VMEM((PANEL, tile), BF16 if share2 % 16 == 0 else F32),
                ],
            ),
            name="level12",
        )(all_maps, *planes, left1, inverse1, left2, inverse2)

    def place(pieces, blocks, slab):
        count = len(pieces)
        whole = [] if slab is None else [slab]
        return pl.pallas_call(
            functools.partial(place_kernel, keep, count),
            out_shape=jax.ShapeDtypeStruct((rows, cols), BF16),
            grid_spec=pltpu.PrefetchScalarGridSpec(
                num_scalar_prefetch=1,
                grid=(count,),
                in_specs=[pl.BlockSpec((last, side), lambda i, meta: (0, 0))] * count + [anywhere()] * len(whole),
                out_specs=pl.BlockSpec((rows, side), lambda i, meta: (0, meta[i])),
            ),
            input_output_aliases={count + 1: 0} if whole else {},
            name="place",
        )(blocks, *pieces, *whole)

    slab = None
    for k in range(chunks):
        give = level0(k, 1 - half)
        from1, from3 = xor_leaf(give, group), xor_leaf(give, 3 * group)
        stay = level0(k, half)
        from2 = xor_leaf(stay, 2 * group)
        done = level12([stay, from1, from2, from3])
        pieces, blocks = [], []
        for r in range(2 * group):
            source = leaf ^ r
            pieces.append(done[r] if r == 0 else xor_leaf(done[r], r))
            column = (source % group) * span + k * chunk + ((source // group) & 1) * side
            blocks.append(column // side)
        slab = place(pieces, jnp.stack(blocks).astype(jnp.int32), slab)
    return slab


def solution(mesh):
    placed = (P("leaf", "panel"), P(None, "leaf", None), P(None, "leaf", None), P())
    return jax.shard_map(
        on_device, mesh=mesh, in_specs=placed, out_specs=P("leaf", "panel"), check_vma=False
    )
```

```python
import functools

import jax
import jax.numpy as jnp
from jax import lax
from jax.experimental import pallas as pl
from jax.experimental.pallas import tpu as pltpu
from jax.sharding import PartitionSpec as P


PANEL = 512
BLOCK = 128
MAP_ROWS = 16
MAP_COLS = 12
CHUNKS = 2
TILE = 256

F32 = jnp.float32
BF16 = jnp.bfloat16


def xor_leaf(block, mask):
    count = lax.axis_size("leaf")
    return lax.ppermute(block, "leaf", [(i, i ^ mask) for i in range(count)])


def dot(a, b):
    return jnp.dot(a, b, preferred_element_type=F32)


def vmem():
    return pl.BlockSpec(memory_space=pltpu.VMEM)


def smem():
    return pl.BlockSpec(memory_space=pltpu.SMEM)


def anywhere():
    return pl.BlockSpec(memory_space=pl.ANY)


def block_at(index):
    return pl.ds(pl.multiple_of(index * BLOCK, BLOCK), BLOCK)


def own_at(level, slot):
    return 2 * level + slot


def cross_at(level, slot):
    return 6 + 2 * level + slot


def lead_level0_kernel(share, maps, near, inverse, left, seed, pivots):
    group = near.shape[0]
    rows = 2 * BLOCK
    rest = rows - share
    for r in range(group):
        sibling = r ^ (group // 2)
        for s in range(2):
            own = near[r, block_at(maps[r, own_at(0, s)]), :].astype(F32)
            cross = near[sibling, block_at(maps[r, cross_at(0, s)]), :].astype(F32)
            summed = (own + cross).astype(BF16)
            if s == 0:
                pivots[r * share:(r + 1) * share, :] = summed[:share]
                if share < BLOCK:
                    left[r * rest:r * rest + BLOCK - share, :] = summed[share:]
            else:
                left[r * rest + BLOCK - share:(r + 1) * rest, :] = summed
    upper = dot(inverse[...], pivots[...]).astype(BF16)
    mine = left[0:rest, :]
    seed[...] = (mine.astype(F32) - dot(mine, upper)).astype(BF16)


def lead_level12_kernel(gone, share, keep, parts, meta, maps, *refs):
    gathered = refs[:parts]
    inverse, left1, left2, front, pivots, upper, sems = refs[parts:]
    group, planes = gathered[0].shape[0], gathered[0].shape[1]
    width = gathered[0].shape[3]
    slabs = group * planes
    rows = 2 * BLOCK
    rest = rows - share
    last = rows - keep
    copies = []
    for i in range(parts):
        column = pl.multiple_of((meta[0] ^ i) * width, width)
        for h in range(planes):
            copy = pltpu.make_async_copy(
                gathered[i].at[:, h, pl.ds(0, rows - gone), :],
                front.at[pl.ds(h * group, group), pl.ds(gone, rows - gone), pl.ds(column, width)],
                sems.at[i * planes + h],
            )
            copy.start()
            copies.append(copy)
    front[:, 0:gone, :] = jnp.zeros((slabs, gone, PANEL), BF16)
    for copy in copies:
        copy.wait()

    def extend1(slab, carry):
        sibling = slab ^ group
        base = slab * rest
        for s in range(2):
            own = front[slab, block_at(maps[slab, own_at(1, s)]), :].astype(F32)
            cross = front[sibling, block_at(maps[slab, cross_at(1, s)]), :].astype(F32)
            summed = (own + cross).astype(BF16)
            if s == 0:
                pivots[pl.ds(pl.multiple_of(slab * share, 16), share), :] = summed[:share]
                left1[pl.ds(pl.multiple_of(base, 16), BLOCK - share), :] = summed[share:]
            else:
                left1[pl.ds(pl.multiple_of(base + BLOCK - share, 16), BLOCK), :] = summed
        return carry

    lax.fori_loop(0, slabs, extend1, 0)
    for half in range(2):
        upper[...] = dot(inverse[half], pivots[half * PANEL:(half + 1) * PANEL, :]).astype(BF16)

        def reduce1(pair, carry):
            first = half * (slabs // 2) + 2 * pair
            mine = left1[pl.ds(pl.multiple_of(first * rest, 16), 2 * rest), :]
            reduced = (mine.astype(F32) - dot(mine, upper[...])).astype(BF16)
            front[first, share:rows, :] = reduced[:rest]
            front[first + 1, share:rows, :] = reduced[rest:]
            return carry

        lax.fori_loop(0, slabs // 4, reduce1, 0)

    def extend2(slab, carry):
        sibling = slab + slabs // 2
        base = slab * last
        for s in range(2):
            own = front[slab, block_at(maps[slab, own_at(2, s)]), :].astype(F32)
            cross = front[sibling, block_at(maps[slab, cross_at(2, s)]), :].astype(F32)
            summed = (own + cross).astype(BF16)
            if s == 0:
                left2[pl.ds(pl.multiple_of(base, 16), BLOCK - keep), :] = summed[keep:]
            else:
                left2[pl.ds(pl.multiple_of(base + BLOCK - keep, 16), BLOCK), :] = summed
        return carry

    lax.fori_loop(0, slabs // 2, extend2, 0)


def level0_kernel(share, meta, maps, *refs):
    group = refs[-1].shape[0]
    slabs = refs[:group]
    left, inverse, out, parent = refs[group:]
    rows = 2 * BLOCK
    rest = rows - share
    tile = out.shape[2]
    for r in range(group):
        sibling = slabs[r ^ (group // 2)]
        for s in range(2):
            own = slabs[r][block_at(maps[r, own_at(0, s)]), :].astype(F32)
            cross = sibling[block_at(maps[r, cross_at(0, s)]), :].astype(F32)
            parent[r, s * BLOCK:(s + 1) * BLOCK, :] = (own + cross).astype(BF16)
    pivots = parent[:, 0:share, :].reshape(PANEL, tile)
    upper = dot(inverse[...], pivots).astype(BF16)
    product = dot(left[...], upper)
    for r in range(group):
        kept = parent[r, share:rows, :].astype(F32)
        out[r, :, :] = (kept - product[r * rest:(r + 1) * rest]).astype(BF16)


def level12_kernel(gone, share, final, keep, maps, *refs):
    planes = refs[:4]
    left1, inverse1, left2, inverse2 = refs[4:8]
    outs = refs[8:-5]
    front, parent, nextf, upper, pivots = refs[-5:]
    group = planes[0].shape[0]
    slabs = 4 * group
    tile = planes[0].shape[2]
    rows = 2 * BLOCK
    rest = rows - share
    last = rows - keep

    @pl.when(pl.program_id(0) == 0)
    def _():
        front[:, 0:gone, :] = jnp.zeros((slabs, gone, tile), BF16)
        nextf[:, 0:share, :] = jnp.zeros((slabs, share, tile), BF16)

    for h in range(4):
        front[h * group:(h + 1) * group, gone:rows, :] = planes[h][...]

    def extend1(slab, carry):
        sibling = slab ^ group
        for s in range(2):
            own = front[slab, block_at(maps[slab, own_at(1, s)]), :].astype(F32)
            cross = front[sibling, block_at(maps[slab, cross_at(1, s)]), :].astype(F32)
            parent[slab, s * BLOCK:(s + 1) * BLOCK, :] = (own + cross).astype(BF16)
        return carry

    lax.fori_loop(0, slabs, extend1, 0)
    for half in range(2):
        taken = parent[half * 2 * group:(half + 1) * 2 * group, 0:share, :].reshape(PANEL, tile)
        upper[...] = dot(inverse1[half], taken).astype(BF16)

        def reduce1(quad, carry):
            first = half * 2 * group + 4 * quad
            product = dot(left1[pl.ds(pl.multiple_of(first * rest, 16), 4 * rest), :], upper[...])
            for i in range(4):
                kept = parent[first + i, share:rows, :].astype(F32)
                nextf[first + i, share:rows, :] = (kept - product[i * rest:(i + 1) * rest]).astype(BF16)
            return carry

        lax.fori_loop(0, group // 2, reduce1, 0)

    def extend2(slab, carry):
        sibling = slab + 2 * group
        for s in range(2):
            own = nextf[slab, block_at(maps[slab, own_at(2, s)]), :].astype(F32)
            cross = nextf[sibling, block_at(maps[slab, cross_at(2, s)]), :].astype(F32)
            parent[slab, s * BLOCK:(s + 1) * BLOCK, :] = (own + cross).astype(BF16)
        return carry

    lax.fori_loop(0, 2 * group, extend2, 0)
    head = max(final, 16)
    for slab in range(slabs):
        if slab < 2 * group:
            taken = parent[slab, 0:head, :]
        else:
            at = pl.multiple_of(maps[slab, own_at(2, 0)] * BLOCK, BLOCK)
            own = nextf[slab, pl.ds(at, head), :].astype(F32)
            at = pl.multiple_of(maps[slab, cross_at(2, 0)] * BLOCK, BLOCK)
            cross = nextf[slab - 2 * group, pl.ds(at, head), :].astype(F32)
            taken = (own + cross).astype(BF16)
        pivots[slab * final:(slab + 1) * final, :] = taken.astype(pivots.dtype)[:final]
    upper[...] = dot(inverse2[...], pivots[...].astype(BF16)).astype(BF16)
    for slab in range(2 * group):
        product = dot(left2[slab * last:(slab + 1) * last, :], upper[...])
        reduced = parent[slab, keep:rows, :].astype(F32) - product
        if keep < final:
            row = lax.broadcasted_iota(jnp.int32, reduced.shape, 0)
            reduced = jnp.where(row >= final - keep, reduced, 0.0)
        outs[slab][...] = reduced.astype(BF16)


def place_kernel(keep, count, meta, *refs):
    pieces, out = refs[:count], refs[-1]
    if keep:
        out[0:keep, :] = jnp.zeros((keep, out.shape[1]), BF16)
    for i, piece in enumerate(pieces):

        @pl.when(pl.program_id(0) == i)
        def _(piece=piece):
            out[keep:, :] = piece[...]


def reordered(inverse, shift):
    index = jnp.arange(PANEL, dtype=jnp.int32)
    table = (index[:, None] == (index[None, :] ^ shift)).astype(BF16)
    return dot(inverse, table).astype(BF16)


def on_device(child_front, own_map, cross_map, pivot_inverse):
    leaf_count = lax.axis_size("leaf")
    panel_count = lax.axis_size("panel")
    leaf = lax.axis_index("leaf")
    panel = lax.axis_index("panel")
    rows, cols = child_front.shape
    group = leaf_count // 4
    member, plane = leaf % group, leaf // group
    half = plane & 1
    share0, share1, share2 = (PANEL // (group << k) for k in range(3))
    keep = share2 // 16 * 16
    span = cols // group
    chunks = min(CHUNKS, span // (2 * BLOCK))
    chunk = span // chunks
    side = chunk // 2
    tile = min(TILE, side)

    maps = jnp.concatenate([own_map[:, 0, :], cross_map[:, 0, :]], axis=0).reshape(1, MAP_COLS)
    map_rows = jnp.pad(maps.astype(BF16), ((0, MAP_ROWS - 1), (0, PANEL - MAP_COLS)))
    lead = jnp.concatenate([child_front[:, :PANEL], map_rows], axis=0)
    near = [lead]
    for r in range(1, group):
        pairs = [(i * panel_count, (i ^ r) * panel_count) for i in range(leaf_count)]
        near.append(lax.ppermute(lead, ("leaf", "panel"), pairs))
    near = jnp.stack(near)
    first = near
    for p in range(1, panel_count):
        copied = lax.ppermute(first, "panel", [(0, p)])
        near = jnp.where(panel == p, copied, near)
    near_maps = near[:, rows, :MAP_COLS].astype(jnp.int32)

    pick = functools.partial(lax.dynamic_index_in_dim, pivot_inverse, axis=0, keepdims=False)
    inverse0 = reordered(pick(plane), member * share0)
    low = (leaf % (2 * group)) * share1
    inverse1 = jnp.stack([reordered(pick(4 + ((plane >> 1) ^ i)), low) for i in range(2)])
    inverse2 = reordered(pivot_inverse[6], leaf * share2)

    received = []
    for k in range(chunks):
        parts = []
        for r in range(1, group):
            start = (member ^ r) * span + k * chunk
            parts.append(xor_leaf(lax.dynamic_slice(child_front, (0, start), (rows, chunk)), r))
        received.append(parts)

    rest0, rest1, last = rows - share0, rows - share1, rows - keep
    left0, seed = pl.pallas_call(
        functools.partial(lead_level0_kernel, share0),
        out_shape=(
            jax.ShapeDtypeStruct((group * rest0, PANEL), BF16),
            jax.ShapeDtypeStruct((rest0, PANEL), BF16),
        ),
        in_specs=[smem(), vmem(), vmem()],
        out_specs=(vmem(), vmem()),
        scratch_shapes=[pltpu.VMEM((PANEL, PANEL), BF16)],
        name="lead0",
    )(near_maps, near, inverse0)

    width = PANEL // panel_count
    piece = lax.dynamic_slice(seed, (0, panel * width), (rest0, width))
    piece = jnp.concatenate([piece, map_rows[:, :width]], axis=0)
    piece = jnp.stack([piece] + [xor_leaf(piece, m * group) for m in range(1, 4)])
    piece = jnp.stack([piece] + [xor_leaf(piece, r) for r in range(1, group)])
    gathered = [piece]
    for i in range(1, panel_count):
        gathered.append(lax.ppermute(piece, "panel", [(p, p ^ i) for p in range(panel_count)]))
    all_maps = piece[:, :, rest0, :MAP_COLS].transpose(1, 0, 2).reshape(leaf_count, MAP_COLS)
    all_maps = all_maps.astype(jnp.int32)

    left1, left2 = pl.pallas_call(
        functools.partial(lead_level12_kernel, share0, share1, keep, panel_count),
        out_shape=(
            jax.ShapeDtypeStruct((leaf_count * rest1, PANEL), BF16),
            jax.ShapeDtypeStruct((2 * group * last, PANEL), BF16),
        ),
        in_specs=[smem(), smem()] + [anywhere()] * panel_count + [vmem()],
        out_specs=(vmem(), vmem()),
        scratch_shapes=[
            pltpu.VMEM((leaf_count, rows, PANEL), BF16),
            pltpu.VMEM((2 * PANEL, PANEL), BF16),
            pltpu.VMEM((PANEL, PANEL), BF16),
            pltpu.SemaphoreType.DMA((4 * panel_count,)),
        ],
        name="lead12",
    )(panel.reshape(1), all_maps, *gathered, inverse1)

    def level0(k, which):
        own_block = (member * span + k * chunk + which * side) // tile
        meta = jnp.stack([own_block, which * (side // tile)]).astype(jnp.int32)
        return pl.pallas_call(
            functools.partial(level0_kernel, share0),
            out_shape=jax.ShapeDtypeStruct((group, rest0, side), BF16),
            grid_spec=pltpu.PrefetchScalarGridSpec(
                num_scalar_prefetch=2,
                grid=(side // tile,),
                in_specs=[pl.BlockSpec((rows, tile), lambda j, meta, maps: (0, meta[0] + j))]
                + [pl.BlockSpec((rows, tile), lambda j, meta, maps: (0, meta[1] + j))] * (group - 1)
                + [
                    pl.BlockSpec((group * rest0, PANEL), lambda j, meta, maps: (0, 0)),
                    pl.BlockSpec((PANEL, PANEL), lambda j, meta, maps: (0, 0)),
                ],
                out_specs=pl.BlockSpec((group, rest0, tile), lambda j, meta, maps: (0, 0, j)),
                scratch_shapes=[pltpu.VMEM((group, rows, tile), BF16)],
            ),
            name="level0",
        )(meta, near_maps, child_front, *received[k], left0, inverse0)

    def level12(planes):
        return pl.pallas_call(
            functools.partial(level12_kernel, share0, share1, share2, keep),
            out_shape=[jax.ShapeDtypeStruct((last, side), BF16)] * (2 * group),
            grid_spec=pltpu.PrefetchScalarGridSpec(
                num_scalar_prefetch=1,
                grid=(side // tile,),
                in_specs=[pl.BlockSpec((group, rest0, tile), lambda j, maps: (0, 0, j))] * 4 + [vmem()] * 4,
                out_specs=[pl.BlockSpec((last, tile), lambda j, maps: (0, j))] * (2 * group),
                scratch_shapes=[
                    pltpu.VMEM((leaf_count, rows, tile), BF16),
                    pltpu.VMEM((leaf_count, rows, tile), BF16),
                    pltpu.VMEM((leaf_count, rows, tile), BF16),
                    pltpu.VMEM((PANEL, tile), BF16),
                    pltpu.VMEM((PANEL, tile), BF16 if share2 % 16 == 0 else F32),
                ],
            ),
            name="level12",
        )(all_maps, *planes, left1, inverse1, left2, inverse2)

    def place(pieces, blocks, slab):
        count = len(pieces)
        whole = [] if slab is None else [slab]
        return pl.pallas_call(
            functools.partial(place_kernel, keep, count),
            out_shape=jax.ShapeDtypeStruct((rows, cols), BF16),
            grid_spec=pltpu.PrefetchScalarGridSpec(
                num_scalar_prefetch=1,
                grid=(count,),
                in_specs=[pl.BlockSpec((last, side), lambda i, meta: (0, 0))] * count + [anywhere()] * len(whole),
                out_specs=pl.BlockSpec((rows, side), lambda i, meta: (0, meta[i])),
            ),
            input_output_aliases={count + 1: 0} if whole else {},
            name="place",
        )(blocks, *pieces, *whole)

    slab = None
    for k in range(chunks):
        give = level0(k, 1 - half)
        from1, from3 = xor_leaf(give, group), xor_leaf(give, 3 * group)
        stay = level0(k, half)
        from2 = xor_leaf(stay, 2 * group)
        done = level12([stay, from1, from2, from3])
        pieces, blocks = [], []
        for r in range(2 * group):
            source = leaf ^ r
            pieces.append(done[r] if r == 0 else xor_leaf(done[r], r))
            column = (source % group) * span + k * chunk + ((source // group) & 1) * side
            blocks.append(column // side)
        slab = place(pieces, jnp.stack(blocks).astype(jnp.int32), slab)
    return slab


def solution(mesh):
    placed = (P("leaf", "panel"), P(None, "leaf", None), P(None, "leaf", None), P())
    return jax.shard_map(
        on_device, mesh=mesh, in_specs=placed, out_specs=P("leaf", "panel"), check_vma=False
    )
```

```python
import functools
import math

import jax
import jax.numpy as jnp
from jax import lax
from jax.experimental import pallas as pl
from jax.experimental.pallas import tpu as pltpu
from jax.sharding import PartitionSpec as P


PANEL = 512
BLOCK = 128
MAP_ROWS = 16
MAP_COLS = 12
SHARES = (1, 2, 1)
APART = (2,)
TILE = 256
FINAL_TILE = 512

F32 = jnp.float32
BF16 = jnp.bfloat16


def xor_leaf(block, mask):
    count = lax.axis_size("leaf")
    return lax.ppermute(block, "leaf", [(i, i ^ mask) for i in range(count)])


def xor_panel(block, mask):
    count = lax.axis_size("panel")
    return lax.ppermute(block, "panel", [(i, i ^ mask) for i in range(count)])


def dot(a, b):
    return jnp.dot(a, b, preferred_element_type=F32)


def room(*shapes):
    total = sum(2 * math.prod(shape) for shape in shapes)
    return pltpu.CompilerParams(vmem_limit_bytes=min(total + (6 << 20), 60 << 20))


def vmem():
    return pl.BlockSpec(memory_space=pltpu.VMEM)


def in_hbm(shape):
    return pltpu.HBM(shape, BF16)


def smem():
    return pl.BlockSpec(memory_space=pltpu.SMEM)


def anywhere():
    return pl.BlockSpec(memory_space=pl.ANY)


def block_at(index):
    return pl.ds(pl.multiple_of(index * BLOCK, BLOCK), BLOCK)


def turn(r, meta, count, share):
    return pl.ds(pl.multiple_of(((r ^ meta[0]) & (count - 1)) * share, share), share)


def own_at(level, slot):
    return 2 * level + slot


def cross_at(level, slot):
    return 6 + 2 * level + slot


def lead_level0_kernel(share, meta, maps, *refs):
    parts = refs[:-6]
    inverse, left, seed, near, pivots, sems = refs[-6:]
    group, width = near.shape[0], parts[0].shape[2]
    copies = []
    for i, part in enumerate(parts):
        column = pl.multiple_of((meta[1] ^ i) * width, width)
        source = part.at[:, pl.ds(0, 2 * BLOCK), :]
        copies.append(pltpu.make_async_copy(source, near.at[:, :, pl.ds(column, width)], sems.at[i]))
    for copy in copies:
        copy.start()
    for copy in copies:
        copy.wait()
    rows = 2 * BLOCK
    rest = rows - share
    for r in range(group):
        sibling = r ^ (group // 2)
        for s in range(2):
            own = near[r, block_at(maps[r, own_at(0, s)]), :]
            cross = near[sibling, block_at(maps[r, cross_at(0, s)]), :]
            summed = own + cross
            if s == 0:
                pivots[turn(r, meta, group, share), :] = summed[:share]
                if share < BLOCK:
                    left[r * rest:r * rest + BLOCK - share, :] = summed[share:]
            else:
                left[r * rest + BLOCK - share:(r + 1) * rest, :] = summed
    upper = dot(inverse[0], pivots[...]).astype(BF16)
    mine = left[0:rest, :]
    seed[...] = (mine.astype(F32) - dot(mine, upper)).astype(BF16)


def lead_level12_kernel(gone, share, keep, parts, meta, maps, *refs):
    gathered = refs[:parts]
    inverses = refs[parts:parts + 2]
    left1, left2, front, pivots, upper, sems = refs[parts + 2:]
    group, planes = gathered[0].shape[0], gathered[0].shape[1]
    width = gathered[0].shape[3]
    slabs = group * planes
    rows = 2 * BLOCK
    rest = rows - share
    last = rows - keep
    copies = []
    for i in range(parts):
        column = pl.multiple_of((meta[1] ^ i) * width, width)
        for h in range(planes):
            copy = pltpu.make_async_copy(
                gathered[i].at[:, h, pl.ds(0, rows - gone), :],
                front.at[pl.ds(h * group, group), pl.ds(gone, rows - gone), pl.ds(column, width)],
                sems.at[i * planes + h],
            )
            copy.start()
            copies.append(copy)
    front[:, 0:gone, :] = jnp.zeros((slabs, gone, PANEL), BF16)
    for copy in copies:
        copy.wait()

    def extend1(slab, carry):
        sibling = slab ^ group
        base = slab * rest
        for s in range(2):
            own = front[slab, block_at(maps[slab, own_at(1, s)]), :]
            cross = front[sibling, block_at(maps[slab, cross_at(1, s)]), :]
            summed = own + cross
            if s == 0:
                pivots[slab // (slabs // 2), turn(slab, meta, slabs // 2, share), :] = summed[:share]
                left1[pl.ds(pl.multiple_of(base, 16), BLOCK - share), :] = summed[share:]
            else:
                left1[pl.ds(pl.multiple_of(base + BLOCK - share, 16), BLOCK), :] = summed
        return carry

    lax.fori_loop(0, slabs, extend1, 0)
    for half in range(2):
        upper[...] = dot(inverses[half][0], pivots[half]).astype(BF16)

        def reduce1(pair, carry):
            first = half * (slabs // 2) + 2 * pair
            mine = left1[pl.ds(pl.multiple_of(first * rest, 16), 2 * rest), :]
            reduced = (mine.astype(F32) - dot(mine, upper[...])).astype(BF16)
            front[first, share:rows, :] = reduced[:rest]
            front[first + 1, share:rows, :] = reduced[rest:]
            return carry

        lax.fori_loop(0, slabs // 4, reduce1, 0)

    def extend2(slab, carry):
        sibling = slab + slabs // 2
        base = slab * last
        for s in range(2):
            own = front[slab, block_at(maps[slab, own_at(2, s)]), :]
            cross = front[sibling, block_at(maps[slab, cross_at(2, s)]), :]
            summed = own + cross
            if s == 0:
                left2[pl.ds(pl.multiple_of(base, 16), BLOCK - keep), :] = summed[keep:]
            else:
                left2[pl.ds(pl.multiple_of(base + BLOCK - keep, 16), BLOCK), :] = summed
        return carry

    lax.fori_loop(0, slabs // 2, extend2, 0)


def level0_kernel(share, meta, maps, *refs):
    give, stay, parent, pivots = refs[-4:]
    group = give.shape[0]
    slabs = refs[:group]
    left, inverse = refs[group:group + 2]
    rows = 2 * BLOCK
    rest = rows - share
    for r in range(group):
        sibling = slabs[r ^ (group // 2)]
        for s in range(2):
            own = slabs[r][block_at(maps[r, own_at(0, s)]), :]
            cross = sibling[block_at(maps[r, cross_at(0, s)]), :]
            parent[r, s * BLOCK:(s + 1) * BLOCK, :] = own + cross
        pivots[turn(r, meta, group, share), :] = parent[r, 0:share, :]
    upper = dot(inverse[0], pivots[...]).astype(BF16)
    product = dot(left[...], upper)

    def write(out):
        for r in range(group):
            kept = parent[r, share:rows, :].astype(F32)
            out[r, :, :] = (kept - product[r * rest:(r + 1) * rest]).astype(BF16)

    first = pl.program_id(0) < pl.num_programs(0) // 2
    pl.when(first)(lambda: write(give))
    pl.when(jnp.logical_not(first))(lambda: write(stay))


def level12_kernel(gone, share, final, keep, meta, maps, *refs):
    planes = refs[:4]
    left1_in, left2_in = refs[4:6]
    inverses = refs[6:9]
    outs = refs[9:-9]
    front, parent, nextf, upper, pivots, finals, left1, left2, sems = refs[-9:]
    group = planes[0].shape[0]
    slabs = 4 * group
    tile = planes[0].shape[2]
    rows = 2 * BLOCK
    rest = rows - share
    last = rows - keep

    load1 = pltpu.make_async_copy(left1_in, left1, sems.at[0])
    load2 = pltpu.make_async_copy(left2_in, left2, sems.at[1])
    opening = pl.program_id(0) == 0

    @pl.when(opening)
    def _():
        load1.start()
        load2.start()
        front[:, 0:gone, :] = jnp.zeros((slabs, gone, tile), BF16)
        nextf[:, 0:share, :] = jnp.zeros((slabs, share, tile), BF16)

    for h in range(4):
        front[h * group:(h + 1) * group, gone:rows, :] = planes[h][...]

    def extend1(slab, carry):
        sibling = slab ^ group
        for s in range(2):
            own = front[slab, block_at(maps[slab, own_at(1, s)]), :]
            cross = front[sibling, block_at(maps[slab, cross_at(1, s)]), :]
            parent[slab, s * BLOCK:(s + 1) * BLOCK, :] = own + cross
        taken = parent[slab, 0:share, :]
        pivots[slab // (2 * group), turn(slab, meta, 2 * group, share), :] = taken
        return carry

    lax.fori_loop(0, slabs, extend1, 0)
    pl.when(opening)(load1.wait)
    for half in range(2):
        upper[...] = dot(inverses[half][0], pivots[half]).astype(BF16)

        def reduce1(quad, carry):
            first = half * 2 * group + 4 * quad
            product = dot(left1[pl.ds(pl.multiple_of(first * rest, 16), 4 * rest), :], upper[...])
            for i in range(4):
                kept = parent[first + i, share:rows, :].astype(F32)
                nextf[first + i, share:rows, :] = (kept - product[i * rest:(i + 1) * rest]).astype(BF16)
            return carry

        lax.fori_loop(0, group // 2, reduce1, 0)

    def extend2(slab, carry):
        sibling = slab + 2 * group
        for s in range(2):
            own = nextf[slab, block_at(maps[slab, own_at(2, s)]), :]
            cross = nextf[sibling, block_at(maps[slab, cross_at(2, s)]), :]
            parent[slab, s * BLOCK:(s + 1) * BLOCK, :] = own + cross
        return carry

    lax.fori_loop(0, 2 * group, extend2, 0)
    head = max(final, 16)
    for slab in range(slabs):
        if slab < 2 * group:
            taken = parent[slab, 0:head, :]
        else:
            at = pl.multiple_of(maps[slab, own_at(2, 0)] * BLOCK, BLOCK)
            own = nextf[slab, pl.ds(at, head), :]
            at = pl.multiple_of(maps[slab, cross_at(2, 0)] * BLOCK, BLOCK)
            taken = own + nextf[slab - 2 * group, pl.ds(at, head), :]
        finals[turn(slab, meta, slabs, final), :] = taken.astype(finals.dtype)[:final]
    upper[...] = dot(inverses[2][0], finals[...].astype(BF16)).astype(BF16)
    pl.when(opening)(load2.wait)
    for slab in range(2 * group):
        product = dot(left2[slab * last:(slab + 1) * last, :], upper[...])
        reduced = parent[slab, keep:rows, :].astype(F32) - product
        if keep < final:
            row = lax.broadcasted_iota(jnp.int32, reduced.shape, 0)
            reduced = jnp.where(row >= final - keep, reduced, 0.0)
        if len(outs) == 1:
            outs[0][(slab ^ meta[0]) & (2 * group - 1), :, :] = reduced.astype(BF16)
        else:
            outs[slab][...] = reduced.astype(BF16)


def place_kernel(keep, count, column, meta, *refs):
    pieces, (out, zeros, sems) = refs[:-3], refs[-3:]
    height, side = pieces[0].shape[-2:]
    copies = []
    for i in range(count):
        piece = pieces[0].at[i] if len(pieces[0].shape) == 3 else pieces[i]
        columns = pl.ds(pl.multiple_of(column(i, meta), side), side)
        copies.append(pltpu.make_async_copy(piece, out.at[pl.ds(keep, height), columns], sems.at[i]))
        if keep:
            copies.append(pltpu.make_async_copy(zeros, out.at[pl.ds(0, keep), columns], sems.at[count + i]))
    if keep:
        zeros[...] = jnp.zeros(zeros.shape, BF16)
    for copy in copies:
        copy.start()
    for copy in copies:
        copy.wait()


def chunk_sizes(span):
    unit = span // sum(SHARES)
    return [unit * share for share in SHARES] if unit % (2 * TILE) == 0 else [span]


def on_device(child_front, own_map, cross_map, pivot_inverse):
    leaf_count = lax.axis_size("leaf")
    panel_count = lax.axis_size("panel")
    leaf = lax.axis_index("leaf")
    panel = lax.axis_index("panel")
    rows, cols = child_front.shape
    group = leaf_count // 4
    member = leaf % group
    share0, share1, share2 = (PANEL // (group << k) for k in range(3))
    keep = share2 // 16 * 16
    span = cols // group
    sizes = chunk_sizes(span)
    starts = [sum(sizes[:k]) for k in range(len(sizes))]
    meta = jnp.stack([leaf, panel]).astype(jnp.int32)
    child_columns = pltpu.with_memory_space_constraint(child_front, pltpu.HBM)
    plane_bits = group.bit_length() - 1

    maps = jnp.concatenate([own_map[:, 0, :], cross_map[:, 0, :]], axis=0).reshape(1, MAP_COLS)
    map_rows = jnp.pad(maps.astype(BF16), ((0, MAP_ROWS - 1), (0, PANEL - MAP_COLS)))
    width = PANEL // panel_count
    part = child_front[:, :width]
    for p in range(1, panel_count):
        copied = lax.ppermute(child_front[:, p * width:(p + 1) * width], "panel", [(0, p)])
        part = jnp.where(panel == p, copied, part)
    part = jnp.concatenate([part, map_rows[:, :width]], axis=0)
    near = jnp.stack([part] + [xor_leaf(part, r) for r in range(1, group)])
    near_maps = near[:, rows, :MAP_COLS].astype(jnp.int32)
    near = [near] + [xor_panel(near, i) for i in range(1, panel_count)]

    received = []
    for k, chunk in enumerate(sizes):
        parts = []
        for r in range(1, group):
            start = (member ^ r) * span + starts[k]
            columns = lax.dynamic_slice(child_front, (0, start), (rows, chunk))
            parts.append(xor_leaf(columns, r))
        received.append(parts)

    rest0, rest1, last = rows - share0, rows - share1, rows - keep

    def inverse_of(front):
        return pl.BlockSpec((1, PANEL, PANEL), lambda j, meta, maps: (front(meta[0] >> plane_bits), 0, 0))

    level1_inverses = [inverse_of(lambda p: 4 + (p >> 1)), inverse_of(lambda p: 5 - (p >> 1))]
    left0, seed = pl.pallas_call(
        functools.partial(lead_level0_kernel, share0),
        out_shape=(
            jax.ShapeDtypeStruct((group * rest0, PANEL), BF16),
            jax.ShapeDtypeStruct((rest0, PANEL), BF16),
        ),
        grid_spec=pltpu.PrefetchScalarGridSpec(
            num_scalar_prefetch=2,
            grid=(1,),
            in_specs=[anywhere()] * panel_count + [inverse_of(lambda p: p)],
            out_specs=(vmem(), vmem()),
            scratch_shapes=[
                pltpu.VMEM((group, rows, PANEL), BF16),
                pltpu.VMEM((PANEL, PANEL), BF16),
                pltpu.SemaphoreType.DMA((panel_count,)),
            ],
        ),
        compiler_params=room((group, rows, PANEL), (group * rest0, PANEL), *[(PANEL, PANEL)] * 4),
        name="lead0",
    )(meta, near_maps, *near, pivot_inverse)

    piece = lax.dynamic_slice(seed, (0, panel * width), (rest0, width))
    piece = jnp.concatenate([piece, map_rows[:, :width]], axis=0)
    piece = jnp.stack([piece] + [xor_leaf(piece, m * group) for m in range(1, 4)])
    piece = jnp.stack([piece] + [xor_leaf(piece, r) for r in range(1, group)])
    gathered = [piece]
    for i in range(1, panel_count):
        gathered.append(xor_panel(piece, i))
    all_maps = piece[:, :, rest0, :MAP_COLS].transpose(1, 0, 2).reshape(leaf_count, MAP_COLS)
    all_maps = all_maps.astype(jnp.int32)

    left1, left2 = pl.pallas_call(
        functools.partial(lead_level12_kernel, share0, share1, keep, panel_count),
        out_shape=(
            jax.ShapeDtypeStruct((leaf_count * rest1, PANEL), BF16),
            jax.ShapeDtypeStruct((2 * group * last, PANEL), BF16),
        ),
        grid_spec=pltpu.PrefetchScalarGridSpec(
            num_scalar_prefetch=2,
            grid=(1,),
            in_specs=[anywhere()] * panel_count + level1_inverses,
            out_specs=(vmem(), vmem()),
            scratch_shapes=[
                pltpu.VMEM((leaf_count, rows, PANEL), BF16),
                pltpu.VMEM((2, PANEL, PANEL), BF16),
                pltpu.VMEM((PANEL, PANEL), BF16),
                pltpu.SemaphoreType.DMA((4 * panel_count,)),
            ],
        ),
        compiler_params=room(
            (leaf_count * (rows + rest1) + 2 * group * last, PANEL), *[(PANEL, PANEL)] * 7
        ),
        name="lead12",
    )(meta, all_maps, *gathered, pivot_inverse, pivot_inverse)

    def level0(k):
        side = sizes[k] // 2
        tile = min(TILE, side)
        count = side // tile

        def column(j, meta):
            odd = (meta[0] >> plane_bits) & 1
            return jnp.where(j < count, (1 - odd) * count + j, odd * count + j - count)

        def own_column(j, meta, maps):
            base = (meta[0] & (group - 1)) * (span // tile) + starts[k] // tile
            return 0, base + column(j, meta)

        return pl.pallas_call(
            functools.partial(level0_kernel, share0),
            out_shape=[jax.ShapeDtypeStruct((group, rest0, side), BF16)] * 2,
            grid_spec=pltpu.PrefetchScalarGridSpec(
                num_scalar_prefetch=2,
                grid=(2 * count,),
                in_specs=[pl.BlockSpec((rows, tile), own_column)]
                + [pl.BlockSpec((rows, tile), lambda j, meta, maps: (0, column(j, meta)))] * (group - 1)
                + [
                    pl.BlockSpec((group * rest0, PANEL), lambda j, meta, maps: (0, 0)),
                    inverse_of(lambda p: p),
                ],
                out_specs=[
                    pl.BlockSpec((group, rest0, tile), lambda j, meta, maps: (0, 0, jnp.minimum(j, count - 1))),
                    pl.BlockSpec((group, rest0, tile), lambda j, meta, maps: (0, 0, jnp.maximum(j - count, 0))),
                ],
                scratch_shapes=[pltpu.VMEM((group, rows, tile), BF16), pltpu.VMEM((PANEL, tile), BF16)],
            ),
            compiler_params=room(
                (7 * group * rows, tile), (2 * group * rest0, PANEL), *[(PANEL, PANEL)] * 2, (PANEL, 4 * tile)
            ),
            name="level0",
        )(meta, near_maps, child_columns, *received[k], left0, pivot_inverse)

    def level12(planes, apart):
        side = planes[0].shape[2]
        tile = min(FINAL_TILE, side)
        return pl.pallas_call(
            functools.partial(level12_kernel, share0, share1, share2, keep),
            out_shape=[in_hbm((last, side))] * (2 * group) if apart else [in_hbm((2 * group, last, side))],
            grid_spec=pltpu.PrefetchScalarGridSpec(
                num_scalar_prefetch=2,
                grid=(side // tile,),
                in_specs=[pl.BlockSpec((group, rest0, tile), lambda j, meta, maps: (0, 0, j))] * 4
                + [anywhere()] * 2
                + level1_inverses
                + [inverse_of(lambda p: 6)],
                out_specs=[pl.BlockSpec((last, tile), lambda j, meta, maps: (0, j))] * (2 * group)
                if apart
                else [pl.BlockSpec((2 * group, last, tile), lambda j, meta, maps: (0, 0, j))],
                scratch_shapes=[
                    pltpu.VMEM((leaf_count, rows, tile), BF16),
                    pltpu.VMEM((leaf_count, rows, tile), BF16),
                    pltpu.VMEM((leaf_count, rows, tile), BF16),
                    pltpu.VMEM((PANEL, tile), BF16),
                    pltpu.VMEM((2, PANEL, tile), BF16),
                    pltpu.VMEM((PANEL, tile), BF16 if share2 % 16 == 0 else F32),
                    pltpu.VMEM((leaf_count * rest1, PANEL), BF16),
                    pltpu.VMEM((2 * group * last, PANEL), BF16),
                    pltpu.SemaphoreType.DMA((2,)),
                ],
            ),
            compiler_params=room(
                (3 * leaf_count * rows + 8 * group * rest0 + 4 * group * last, tile),
                (leaf_count * rest1 + 2 * group * last, PANEL),
                *[(PANEL, PANEL)] * 6,
                (16 * PANEL, tile),
            ),
            name="level12",
        )(meta, all_maps, *planes, left1, left2, *[pivot_inverse] * 3)

    def place(k, pieces, slab):
        side = sizes[k] // 2
        whole = [] if slab is None else [slab]

        def column(i, meta):
            source = i if len(pieces) == 1 else meta[0] ^ i
            odd = (source >> plane_bits) & 1
            return (source & (group - 1)) * span + starts[k] + odd * side

        return pl.pallas_call(
            functools.partial(place_kernel, keep, 2 * group, column),
            out_shape=jax.ShapeDtypeStruct((rows, cols), BF16),
            in_specs=[smem()] + [vmem()] * len(pieces) + [anywhere()] * len(whole),
            out_specs=anywhere(),
            scratch_shapes=[
                pltpu.VMEM((max(keep, 16), side), BF16),
                pltpu.SemaphoreType.DMA((4 * group,)),
            ],
            input_output_aliases={1 + len(pieces): 0} if whole else {},
            compiler_params=room((2 * group, last, side), (max(keep, 16), side)),
            name="place",
        )(meta, *pieces, *whole)

    pairs = [[base + i for i in range(2 * group)] for base in (0, 2 * group)]
    slab = None
    for k in range(len(sizes)):
        give, stay = level0(k)
        from1, from3 = (xor_leaf(give, m * group) for m in (1, 3))
        from2 = xor_leaf(stay, 2 * group)
        apart = k in APART
        done = level12([stay, from1, from2, from3], apart)
        if apart:
            pieces = [done[0]] + [xor_leaf(done[r], r) for r in range(1, 2 * group)]
        else:
            pieces = [lax.all_to_all(done[0], "leaf", 0, 0, axis_index_groups=pairs, tiled=True)]
        slab = place(k, pieces, slab)
    return slab


def solution(mesh):
    placed = (P("leaf", "panel"), P(None, "leaf", None), P(None, "leaf", None), P())
    return jax.shard_map(on_device, mesh=mesh, in_specs=placed, out_specs=P("leaf", "panel"), check_vma=False)
```

```python
import functools
import math

import jax
import jax.numpy as jnp
from jax import lax
from jax.experimental import pallas as pl
from jax.experimental.pallas import tpu as pltpu
from jax.sharding import PartitionSpec as P


PANEL = 512
BLOCK = 128
MAP_ROWS = 16
MAP_COLS = 12
SHARES = (1, 1, 1, 1)
APART = (1, 2,)
TILE = 256
FINAL_TILE = 512

F32 = jnp.float32
BF16 = jnp.bfloat16


def xor_leaf(block, mask):
    count = lax.axis_size("leaf")
    return lax.ppermute(block, "leaf", [(i, i ^ mask) for i in range(count)])


def xor_panel(block, mask):
    count = lax.axis_size("panel")
    return lax.ppermute(block, "panel", [(i, i ^ mask) for i in range(count)])


def dot(a, b):
    return jnp.dot(a, b, preferred_element_type=F32)


def room(*shapes):
    total = sum(2 * math.prod(shape) for shape in shapes)
    return pltpu.CompilerParams(vmem_limit_bytes=min(total + (6 << 20), 60 << 20))


def vmem():
    return pl.BlockSpec(memory_space=pltpu.VMEM)


def in_hbm(shape):
    return pltpu.HBM(shape, BF16)


def smem():
    return pl.BlockSpec(memory_space=pltpu.SMEM)


def anywhere():
    return pl.BlockSpec(memory_space=pl.ANY)


def block_at(index):
    return pl.ds(pl.multiple_of(index * BLOCK, BLOCK), BLOCK)


def turn(r, meta, count, share):
    return pl.ds(pl.multiple_of(((r ^ meta[0]) & (count - 1)) * share, share), share)


def own_at(level, slot):
    return 2 * level + slot


def cross_at(level, slot):
    return 6 + 2 * level + slot


def lead_level0_kernel(share, meta, maps, *refs):
    parts = refs[:-6]
    inverse, left, seed, near, pivots, sems = refs[-6:]
    group, width = near.shape[0], parts[0].shape[2]
    copies = []
    for i, part in enumerate(parts):
        column = pl.multiple_of((meta[1] ^ i) * width, width)
        source = part.at[:, pl.ds(0, 2 * BLOCK), :]
        copies.append(pltpu.make_async_copy(source, near.at[:, :, pl.ds(column, width)], sems.at[i]))
    for copy in copies:
        copy.start()
    for copy in copies:
        copy.wait()
    rows = 2 * BLOCK
    rest = rows - share
    for r in range(group):
        sibling = r ^ (group // 2)
        for s in range(2):
            own = near[r, block_at(maps[r, own_at(0, s)]), :]
            cross = near[sibling, block_at(maps[r, cross_at(0, s)]), :]
            summed = own + cross
            if s == 0:
                pivots[turn(r, meta, group, share), :] = summed[:share]
                if share < BLOCK:
                    left[r * rest:r * rest + BLOCK - share, :] = summed[share:]
            else:
                left[r * rest + BLOCK - share:(r + 1) * rest, :] = summed
    upper = dot(inverse[0], pivots[...]).astype(BF16)
    mine = left[0:rest, :]
    seed[...] = (mine.astype(F32) - dot(mine, upper)).astype(BF16)


def lead_level12_kernel(gone, share, keep, parts, meta, maps, *refs):
    gathered = refs[:parts]
    inverses = refs[parts:parts + 2]
    left1, left2, front, pivots, upper, sems = refs[parts + 2:]
    group, planes = gathered[0].shape[0], gathered[0].shape[1]
    width = gathered[0].shape[3]
    slabs = group * planes
    rows = 2 * BLOCK
    rest = rows - share
    last = rows - keep
    copies = []
    for i in range(parts):
        column = pl.multiple_of((meta[1] ^ i) * width, width)
        for h in range(planes):
            copy = pltpu.make_async_copy(
                gathered[i].at[:, h, pl.ds(0, rows - gone), :],
                front.at[pl.ds(h * group, group), pl.ds(gone, rows - gone), pl.ds(column, width)],
                sems.at[i * planes + h],
            )
            copy.start()
            copies.append(copy)
    front[:, 0:gone, :] = jnp.zeros((slabs, gone, PANEL), BF16)
    for copy in copies:
        copy.wait()

    def extend1(slab, carry):
        sibling = slab ^ group
        base = slab * rest
        for s in range(2):
            own = front[slab, block_at(maps[slab, own_at(1, s)]), :]
            cross = front[sibling, block_at(maps[slab, cross_at(1, s)]), :]
            summed = own + cross
            if s == 0:
                pivots[slab // (slabs // 2), turn(slab, meta, slabs // 2, share), :] = summed[:share]
                left1[pl.ds(pl.multiple_of(base, 16), BLOCK - share), :] = summed[share:]
            else:
                left1[pl.ds(pl.multiple_of(base + BLOCK - share, 16), BLOCK), :] = summed
        return carry

    lax.fori_loop(0, slabs, extend1, 0)
    for half in range(2):
        upper[...] = dot(inverses[half][0], pivots[half]).astype(BF16)

        def reduce1(pair, carry):
            first = half * (slabs // 2) + 2 * pair
            mine = left1[pl.ds(pl.multiple_of(first * rest, 16), 2 * rest), :]
            reduced = (mine.astype(F32) - dot(mine, upper[...])).astype(BF16)
            front[first, share:rows, :] = reduced[:rest]
            front[first + 1, share:rows, :] = reduced[rest:]
            return carry

        lax.fori_loop(0, slabs // 4, reduce1, 0)

    def extend2(slab, carry):
        sibling = slab + slabs // 2
        base = slab * last
        for s in range(2):
            own = front[slab, block_at(maps[slab, own_at(2, s)]), :]
            cross = front[sibling, block_at(maps[slab, cross_at(2, s)]), :]
            summed = own + cross
            if s == 0:
                left2[pl.ds(pl.multiple_of(base, 16), BLOCK - keep), :] = summed[keep:]
            else:
                left2[pl.ds(pl.multiple_of(base + BLOCK - keep, 16), BLOCK), :] = summed
        return carry

    lax.fori_loop(0, slabs // 2, extend2, 0)


def level0_kernel(share, meta, maps, *refs):
    give, stay, parent, pivots = refs[-4:]
    group = give.shape[0]
    slabs = refs[:group]
    left, inverse = refs[group:group + 2]
    rows = 2 * BLOCK
    rest = rows - share
    for r in range(group):
        sibling = slabs[r ^ (group // 2)]
        for s in range(2):
            own = slabs[r][block_at(maps[r, own_at(0, s)]), :]
            cross = sibling[block_at(maps[r, cross_at(0, s)]), :]
            parent[r, s * BLOCK:(s + 1) * BLOCK, :] = own + cross
        pivots[turn(r, meta, group, share), :] = parent[r, 0:share, :]
    upper = dot(inverse[0], pivots[...]).astype(BF16)
    product = dot(left[...], upper)

    def write(out):
        for r in range(group):
            kept = parent[r, share:rows, :].astype(F32)
            out[r, :, :] = (kept - product[r * rest:(r + 1) * rest]).astype(BF16)

    first = pl.program_id(0) < pl.num_programs(0) // 2
    pl.when(first)(lambda: write(give))
    pl.when(jnp.logical_not(first))(lambda: write(stay))


def level12_kernel(gone, share, final, keep, meta, maps, *refs):
    planes = refs[:4]
    left1_in, left2_in, inverse_in = refs[4:7]
    outs = refs[7:-10]
    front, parent, nextf, upper, pivots, finals, left1, left2, inverses, sems = refs[-10:]
    group = planes[0].shape[0]
    slabs = 4 * group
    tile = planes[0].shape[2]
    rows = 2 * BLOCK
    rest = rows - share
    last = rows - keep

    high = (meta[0] // group) >> 1
    loads = [
        pltpu.make_async_copy(inverse_in.at[index], inverses.at[i], sems.at[2 + i])
        for i, index in enumerate((4 + high, 5 - high, 6))
    ]
    load1 = pltpu.make_async_copy(left1_in, left1, sems.at[0])
    load2 = pltpu.make_async_copy(left2_in, left2, sems.at[1])
    opening = pl.program_id(0) == 0

    @pl.when(opening)
    def _():
        loads[0].start()
        loads[1].start()
        load1.start()
        loads[2].start()
        load2.start()
        front[:, 0:gone, :] = jnp.zeros((slabs, gone, tile), BF16)
        nextf[:, 0:share, :] = jnp.zeros((slabs, share, tile), BF16)

    for h in range(4):
        front[h * group:(h + 1) * group, gone:rows, :] = planes[h][...]

    def extend1(slab, carry):
        sibling = slab ^ group
        for s in range(2):
            own = front[slab, block_at(maps[slab, own_at(1, s)]), :]
            cross = front[sibling, block_at(maps[slab, cross_at(1, s)]), :]
            parent[slab, s * BLOCK:(s + 1) * BLOCK, :] = own + cross
        taken = parent[slab, 0:share, :]
        pivots[slab // (2 * group), turn(slab, meta, 2 * group, share), :] = taken
        return carry

    lax.fori_loop(0, slabs, extend1, 0)
    for half in range(2):
        pl.when(opening)(loads[half].wait)
        upper[...] = dot(inverses[half], pivots[half]).astype(BF16)
        if half == 0:
            pl.when(opening)(load1.wait)

        def reduce1(quad, carry):
            first = half * 2 * group + 4 * quad
            product = dot(left1[pl.ds(pl.multiple_of(first * rest, 16), 4 * rest), :], upper[...])
            for i in range(4):
                kept = parent[first + i, share:rows, :].astype(F32)
                nextf[first + i, share:rows, :] = (kept - product[i * rest:(i + 1) * rest]).astype(BF16)
            return carry

        lax.fori_loop(0, group // 2, reduce1, 0)

    def extend2(slab, carry):
        sibling = slab + 2 * group
        for s in range(2):
            own = nextf[slab, block_at(maps[slab, own_at(2, s)]), :]
            cross = nextf[sibling, block_at(maps[slab, cross_at(2, s)]), :]
            parent[slab, s * BLOCK:(s + 1) * BLOCK, :] = own + cross
        return carry

    lax.fori_loop(0, 2 * group, extend2, 0)
    head = max(final, 16)
    for slab in range(slabs):
        if slab < 2 * group:
            taken = parent[slab, 0:head, :]
        else:
            at = pl.multiple_of(maps[slab, own_at(2, 0)] * BLOCK, BLOCK)
            own = nextf[slab, pl.ds(at, head), :]
            at = pl.multiple_of(maps[slab, cross_at(2, 0)] * BLOCK, BLOCK)
            taken = own + nextf[slab - 2 * group, pl.ds(at, head), :]
        finals[turn(slab, meta, slabs, final), :] = taken.astype(finals.dtype)[:final]
    pl.when(opening)(loads[2].wait)
    upper[...] = dot(inverses[2], finals[...].astype(BF16)).astype(BF16)
    pl.when(opening)(load2.wait)
    for slab in range(2 * group):
        product = dot(left2[slab * last:(slab + 1) * last, :], upper[...])
        reduced = parent[slab, keep:rows, :].astype(F32) - product
        if keep < final:
            row = lax.broadcasted_iota(jnp.int32, reduced.shape, 0)
            reduced = jnp.where(row >= final - keep, reduced, 0.0)
        if len(outs) == 1:
            outs[0][(slab ^ meta[0]) & (2 * group - 1), :, :] = reduced.astype(BF16)
        else:
            outs[slab][...] = reduced.astype(BF16)


def place_kernel(keep, count, column, meta, *refs):
    pieces, (out, zeros, sems) = refs[:-3], refs[-3:]
    height, side = pieces[0].shape[-2:]
    copies = []
    for i in range(count):
        piece = pieces[0].at[i] if len(pieces[0].shape) == 3 else pieces[i]
        columns = pl.ds(pl.multiple_of(column(i, meta), side), side)
        copies.append(pltpu.make_async_copy(piece, out.at[pl.ds(keep, height), columns], sems.at[i]))
        if keep:
            copies.append(pltpu.make_async_copy(zeros, out.at[pl.ds(0, keep), columns], sems.at[count + i]))
    if keep:
        zeros[...] = jnp.zeros(zeros.shape, BF16)
    for copy in copies:
        copy.start()
    for copy in copies:
        copy.wait()


def chunk_sizes(span):
    unit = span // sum(SHARES)
    return [unit * share for share in SHARES] if unit % (2 * TILE) == 0 else [span]


def on_device(child_front, own_map, cross_map, pivot_inverse):
    leaf_count = lax.axis_size("leaf")
    panel_count = lax.axis_size("panel")
    leaf = lax.axis_index("leaf")
    panel = lax.axis_index("panel")
    rows, cols = child_front.shape
    group = leaf_count // 4
    member = leaf % group
    share0, share1, share2 = (PANEL // (group << k) for k in range(3))
    keep = share2 // 16 * 16
    span = cols // group
    sizes = chunk_sizes(span)
    starts = [sum(sizes[:k]) for k in range(len(sizes))]
    meta = jnp.stack([leaf, panel]).astype(jnp.int32)
    inverse_hbm = pltpu.with_memory_space_constraint(pivot_inverse, pltpu.HBM)
    child_columns = pltpu.with_memory_space_constraint(child_front, pltpu.HBM)
    plane_bits = group.bit_length() - 1

    maps = jnp.concatenate([own_map[:, 0, :], cross_map[:, 0, :]], axis=0).reshape(1, MAP_COLS)
    map_rows = jnp.pad(maps.astype(BF16), ((0, MAP_ROWS - 1), (0, PANEL - MAP_COLS)))
    width = PANEL // panel_count
    part = child_front[:, :width]
    for p in range(1, panel_count):
        copied = lax.ppermute(child_front[:, p * width:(p + 1) * width], "panel", [(0, p)])
        part = jnp.where(panel == p, copied, part)
    part = jnp.concatenate([part, map_rows[:, :width]], axis=0)
    near = jnp.stack([part] + [xor_leaf(part, r) for r in range(1, group)])
    near_maps = near[:, rows, :MAP_COLS].astype(jnp.int32)
    near = [near] + [xor_panel(near, i) for i in range(1, panel_count)]

    received = []
    for k, chunk in enumerate(sizes):
        parts = []
        for r in range(1, group):
            start = (member ^ r) * span + starts[k]
            columns = lax.dynamic_slice(child_front, (0, start), (rows, chunk))
            parts.append(xor_leaf(columns, r))
        received.append(parts)

    rest0, rest1, last = rows - share0, rows - share1, rows - keep

    def inverse_of(front):
        return pl.BlockSpec((1, PANEL, PANEL), lambda j, meta, maps: (front(meta[0] >> plane_bits), 0, 0))

    level1_inverses = [inverse_of(lambda p: 4 + (p >> 1)), inverse_of(lambda p: 5 - (p >> 1))]
    left0, seed = pl.pallas_call(
        functools.partial(lead_level0_kernel, share0),
        out_shape=(
            jax.ShapeDtypeStruct((group * rest0, PANEL), BF16),
            jax.ShapeDtypeStruct((rest0, PANEL), BF16),
        ),
        grid_spec=pltpu.PrefetchScalarGridSpec(
            num_scalar_prefetch=2,
            grid=(1,),
            in_specs=[anywhere()] * panel_count + [inverse_of(lambda p: p)],
            out_specs=(vmem(), vmem()),
            scratch_shapes=[
                pltpu.VMEM((group, rows, PANEL), BF16),
                pltpu.VMEM((PANEL, PANEL), BF16),
                pltpu.SemaphoreType.DMA((panel_count,)),
            ],
        ),
        compiler_params=room((group, rows, PANEL), (group * rest0, PANEL), *[(PANEL, PANEL)] * 4),
        name="lead0",
    )(meta, near_maps, *near, inverse_hbm)

    piece = lax.dynamic_slice(seed, (0, panel * width), (rest0, width))
    piece = jnp.concatenate([piece, map_rows[:, :width]], axis=0)
    piece = jnp.stack([piece] + [xor_leaf(piece, m * group) for m in range(1, 4)])
    piece = jnp.stack([piece] + [xor_leaf(piece, r) for r in range(1, group)])
    gathered = [piece]
    for i in range(1, panel_count):
        gathered.append(xor_panel(piece, i))
    all_maps = piece[:, :, rest0, :MAP_COLS].transpose(1, 0, 2).reshape(leaf_count, MAP_COLS)
    all_maps = all_maps.astype(jnp.int32)

    left1, left2 = pl.pallas_call(
        functools.partial(lead_level12_kernel, share0, share1, keep, panel_count),
        out_shape=(
            jax.ShapeDtypeStruct((leaf_count * rest1, PANEL), BF16),
            jax.ShapeDtypeStruct((2 * group * last, PANEL), BF16),
        ),
        grid_spec=pltpu.PrefetchScalarGridSpec(
            num_scalar_prefetch=2,
            grid=(1,),
            in_specs=[anywhere()] * panel_count + level1_inverses,
            out_specs=(vmem(), vmem()),
            scratch_shapes=[
                pltpu.VMEM((leaf_count, rows, PANEL), BF16),
                pltpu.VMEM((2, PANEL, PANEL), BF16),
                pltpu.VMEM((PANEL, PANEL), BF16),
                pltpu.SemaphoreType.DMA((4 * panel_count,)),
            ],
        ),
        compiler_params=room(
            (leaf_count * (rows + rest1) + 2 * group * last, PANEL), *[(PANEL, PANEL)] * 7
        ),
        name="lead12",
    )(meta, all_maps, *gathered, pivot_inverse, pivot_inverse)

    def level0(k):
        side = sizes[k] // 2
        tile = min(TILE, side)
        count = side // tile

        def column(j, meta):
            odd = (meta[0] >> plane_bits) & 1
            return jnp.where(j < count, (1 - odd) * count + j, odd * count + j - count)

        def own_column(j, meta, maps):
            base = (meta[0] & (group - 1)) * (span // tile) + starts[k] // tile
            return 0, base + column(j, meta)

        return pl.pallas_call(
            functools.partial(level0_kernel, share0),
            out_shape=[jax.ShapeDtypeStruct((group, rest0, side), BF16)] * 2,
            grid_spec=pltpu.PrefetchScalarGridSpec(
                num_scalar_prefetch=2,
                grid=(2 * count,),
                in_specs=[pl.BlockSpec((rows, tile), own_column)]
                + [pl.BlockSpec((rows, tile), lambda j, meta, maps: (0, column(j, meta)))] * (group - 1)
                + [
                    pl.BlockSpec((group * rest0, PANEL), lambda j, meta, maps: (0, 0)),
                    inverse_of(lambda p: p),
                ],
                out_specs=[
                    pl.BlockSpec((group, rest0, tile), lambda j, meta, maps: (0, 0, jnp.minimum(j, count - 1))),
                    pl.BlockSpec((group, rest0, tile), lambda j, meta, maps: (0, 0, jnp.maximum(j - count, 0))),
                ],
                scratch_shapes=[pltpu.VMEM((group, rows, tile), BF16), pltpu.VMEM((PANEL, tile), BF16)],
            ),
            compiler_params=room(
                (7 * group * rows, tile), (2 * group * rest0, PANEL), *[(PANEL, PANEL)] * 2, (PANEL, 4 * tile)
            ),
            name="level0",
        )(meta, near_maps, child_columns, *received[k], left0, inverse_hbm)

    def level12(planes, apart):
        side = planes[0].shape[2]
        tile = min(FINAL_TILE, side)
        return pl.pallas_call(
            functools.partial(level12_kernel, share0, share1, share2, keep),
            out_shape=[in_hbm((last, side))] * (2 * group) if apart else [in_hbm((2 * group, last, side))],
            grid_spec=pltpu.PrefetchScalarGridSpec(
                num_scalar_prefetch=2,
                grid=(side // tile,),
                in_specs=[pl.BlockSpec((group, rest0, tile), lambda j, meta, maps: (0, 0, j))] * 4
                + [anywhere()] * 2
                + [pl.BlockSpec(memory_space=pltpu.HBM)],
                out_specs=[pl.BlockSpec((last, tile), lambda j, meta, maps: (0, j))] * (2 * group)
                if apart
                else [pl.BlockSpec((2 * group, last, tile), lambda j, meta, maps: (0, 0, j))],
                scratch_shapes=[
                    pltpu.VMEM((leaf_count, rows, tile), BF16),
                    pltpu.VMEM((leaf_count, rows, tile), BF16),
                    pltpu.VMEM((leaf_count, rows, tile), BF16),
                    pltpu.VMEM((PANEL, tile), BF16),
                    pltpu.VMEM((2, PANEL, tile), BF16),
                    pltpu.VMEM((PANEL, tile), BF16 if share2 % 16 == 0 else F32),
                    pltpu.VMEM((leaf_count * rest1, PANEL), BF16),
                    pltpu.VMEM((2 * group * last, PANEL), BF16),
                    pltpu.VMEM((3, PANEL, PANEL), BF16),
                    pltpu.SemaphoreType.DMA((5,)),
                ],
            ),
            compiler_params=room(
                (3 * leaf_count * rows + 8 * group * rest0 + 4 * group * last, tile),
                (leaf_count * rest1 + 2 * group * last, PANEL),
                *[(PANEL, PANEL)] * 3,
                (12 * PANEL, tile),
            ),
            name="level12",
        )(meta, all_maps, *planes, left1, left2, pivot_inverse)

    def place(k, pieces, slab):
        side = sizes[k] // 2
        whole = [] if slab is None else [slab]

        def column(i, meta):
            source = i if len(pieces) == 1 else meta[0] ^ i
            odd = (source >> plane_bits) & 1
            return (source & (group - 1)) * span + starts[k] + odd * side

        return pl.pallas_call(
            functools.partial(place_kernel, keep, 2 * group, column),
            out_shape=jax.ShapeDtypeStruct((rows, cols), BF16),
            in_specs=[smem()] + [vmem()] * len(pieces) + [anywhere()] * len(whole),
            out_specs=anywhere(),
            scratch_shapes=[
                pltpu.VMEM((max(keep, 16), side), BF16),
                pltpu.SemaphoreType.DMA((4 * group,)),
            ],
            input_output_aliases={1 + len(pieces): 0} if whole else {},
            compiler_params=room((2 * group, last, side), (max(keep, 16), side)),
            name="place",
        )(meta, *pieces, *whole)

    pairs = [[base + i for i in range(2 * group)] for base in (0, 2 * group)]
    slab = None
    for k in range(len(sizes)):
        give, stay = level0(k)
        from1, from3 = (xor_leaf(give, m * group) for m in (1, 3))
        from2 = xor_leaf(stay, 2 * group)
        apart = k in APART
        done = level12([stay, from1, from2, from3], apart)
        if apart:
            pieces = [done[0]] + [xor_leaf(done[r], r) for r in range(1, 2 * group)]
        else:
            pieces = [lax.all_to_all(done[0], "leaf", 0, 0, axis_index_groups=pairs, tiled=True)]
        slab = place(k, pieces, slab)
    return slab


def solution(mesh):
    placed = (P("leaf", "panel"), P(None, "leaf", None), P(None, "leaf", None), P())
    return jax.shard_map(on_device, mesh=mesh, in_specs=placed, out_specs=P("leaf", "panel"), check_vma=False)
```
